512 devices in a mesh: dp: 32 (over y, x, core), tensor: 16 (over z).
Axes of the slice: x: 4, y: 4, z: 16, core: 2. Of those that a mesh axis runs over, the one named last changes fastest.
Arguments:
- x_tokens: bfloat16 [2048, 8192], P('dp', 'tensor'), may hold values from -6 to 6
- sign_bits: int32 [8192], P('tensor'), may hold values from 0 to 1
- weight: bfloat16 [8192, 28672], P('tensor', 'dp'), may hold values from -0.0625 to 0.0625
- upstream: bfloat16 [2048, 28672], P('tensor', 'dp'), may hold values from -0.125 to 0.125
Outputs:
- projected: bfloat16 [2048, 28672], P('tensor', 'dp')
- weight_grad: float32 [8192, 28672], P('tensor', 'dp')
The draws below stay inside these ranges and needn't reach their ends.
All inputs are finite; a program needn't handle non-finite values.
Results may differ from the reference program's by a relative error of at most 0.028.
Values may be sent and summed in bfloat16 or wider, within the bound.
A program may use at most 64 MiB of HBM per device.

```python
import math
import jax
import jax.numpy as jnp
from jax import lax

D = 8192
FFW = 28672
TOKENS = 2048
N_TENSOR = 16


def plant(values, stream_key, smallest, top_value):
    longest = values.shape.index(max(values.shape))
    spots = []
    for shift in (0, 1):
        where = [jax.random.randint(jax.random.fold_in(stream_key, axis), (), 0, length) for axis, length in enumerate(values.shape)]
        where[longest] = (where[longest] + shift) % values.shape[longest]
        spots.append(tuple(where))
    return values.at[spots[0]].set(smallest).at[spots[1]].set(top_value)


def levels(stream_key, shape, pieces, low, top_value):
    def one(axis_at, parts):
        heights = jax.random.uniform(jax.random.fold_in(jax.random.fold_in(stream_key, 6), axis_at), (parts,), jnp.float32, low / len(pieces), top_value / len(pieces))
        return jnp.repeat(jnp.exp(heights), shape[axis_at] // parts).reshape((-1,) + (1,) * (len(shape) - axis_at - 1))

    gain = one(*pieces[0])
    for cut in pieces[1:]:
        gain = gain * one(*cut)
    return gain


def noise(rng, extent, width, bound, split=(), held_as=jnp.bfloat16):
    values = width * jax.random.normal(rng, extent, jnp.float32)
    if split:
        values = values * levels(rng, extent, split, -0.22, 0.18)
    return jnp.clip(values, -bound, bound).astype(held_as)


def setup_inputs(seed: int = 0) -> dict:
    key_of = jax.random.split(jax.random.key(seed), 5)
    return {
        "x_tokens": noise(key_of[0], (TOKENS, D), 1.0, 6.0, ((0, 32), (1, 16))),
        "sign_bits": plant(jax.random.randint(key_of[1], (D,), 0, 2), jax.random.fold_in(key_of[1], 1), 0, 1).astype(jnp.int32),
        "weight": noise(key_of[2], (D, FFW), D ** -0.5, 0.0625, ((0, 16), (1, 32))),
        "upstream": noise(key_of[3], (TOKENS, FFW), TOKENS ** -0.5, 0.125, ((0, 16), (1, 32))),
    }


def hadamard(order):
    row_ids = jnp.arange(order, dtype=jnp.int32)[:, None]
    col_ids = jnp.arange(order, dtype=jnp.int32)[None, :]
    common = row_ids & col_ids
    parity = jnp.zeros((order, order), jnp.int32)
    for section_bit in range(max(order.bit_length() - 1, 0)):
        parity = parity + (common >> section_bit & 1)
    return (1 - 2 * (parity % 2)).astype(jnp.float32)

def reference(x_tokens, sign_bits, weight, upstream):
    groups = N_TENSOR
    panel_width = D // N_TENSOR
    column_sign = (1 - 2 * sign_bits).astype(jnp.float32)
    signed = x_tokens.astype(jnp.float32) * column_sign[None, :]
    blocks = signed.reshape(TOKENS, groups, panel_width)
    inner = jnp.einsum('rtd,de->rte', blocks, hadamard(panel_width), precision=lax.Precision.HIGHEST)
    outer = jnp.einsum('rtd,st->rsd', inner, hadamard(groups), precision=lax.Precision.HIGHEST)
    factor = 1.0 / math.sqrt(D)
    quantized = (outer.reshape(TOKENS, D) * factor).astype(jnp.bfloat16)
    q_blocks = quantized.reshape(TOKENS, groups, panel_width).transpose(1, 0, 2)
    w_blocks = weight.reshape(groups, panel_width, FFW)

    def add_group(running, pair):
        partial_value = jnp.dot(pair[0], pair[1], preferred_element_type=jnp.float32).astype(jnp.bfloat16)
        partial_value = lax.optimization_barrier(partial_value)
        return (running + partial_value.astype(jnp.float32), None)
    summed, _ = lax.scan(add_group, jnp.zeros((TOKENS, FFW), jnp.float32), (q_blocks, w_blocks))
    projected = summed.astype(jnp.bfloat16)
    weight_grad = lax.dot_general(quantized, upstream, (((0,), (0,)), ((), ())), preferred_element_type=jnp.float32)
    return (projected, weight_grad)
```

```python
import math

import jax
import jax.numpy as jnp
from jax import lax
from jax.experimental import pallas as pl
from jax.experimental.pallas import tpu as pltpu
from jax.sharding import PartitionSpec as P

MESH = pl.DeviceIdType.MESH
F32 = jnp.float32
BF16 = jnp.bfloat16
NZ = 16
NX = 4
NY = 4
SUB = 2


def hadamard_128():
    rows = lax.broadcasted_iota(jnp.int32, (128, 128), 0)
    cols = lax.broadcasted_iota(jnp.int32, (128, 128), 1)
    bits = rows & cols
    bits = bits ^ (bits >> 4)
    bits = bits ^ (bits >> 2)
    bits = bits ^ (bits >> 1)
    return (1 - 2 * (bits & 1)).astype(F32).astype(BF16)


def butterfly(values):
    values = list(values)
    stride = 1
    while stride < len(values):
        for low in range(len(values)):
            if not low & stride:
                a, b = values[low], values[low | stride]
                values[low], values[low | stride] = a + b, a - b
        stride *= 2
    return values


def kernel(
    x_ref, sign_ref, w_hbm, u_hbm, proj_ref, grad_ref,
    inner, recv1, send2, q, qt, w, uall, part, rbuf, sbuf,
    loc_sem, a1_send, a1_recv, a2_send, a2_recv,
    x_send, x_recv, y_send, y_recv, c_send, c_recv,
    ag_send, ag_recv, rs_send, rs_recv,
):
    me = lax.axis_index("tensor")
    dp = lax.axis_index("dp")
    core = lax.rem(dp, 2)
    chip = lax.div(dp, 2)
    xx = lax.rem(chip, NX)
    yy = lax.div(chip, NX)
    half = q.shape[1] // NZ
    quarter = half * NX

    def z_dev(shift):
        return {"tensor": lax.rem(me + shift + NZ, NZ)}

    def x_dev(shift):
        return {"dp": (yy * NX + lax.rem(xx + shift, NX)) * 2 + core}

    def y_dev(shift):
        return {"dp": (lax.rem(yy + shift, NY) * NX + xx) * 2 + core}

    partner = {"dp": chip * 2 + 1 - core}

    w_copy = pltpu.make_async_copy(w_hbm, w, loc_sem.at[0])
    w_copy.start()
    own_rows = pl.ds(pl.multiple_of(me * half, half), half)
    u_copies = []
    for h in range(2):
        cp = pltpu.make_async_copy(
            u_hbm.at[pl.ds(h * half, half)], uall.at[h, own_rows], loc_sem.at[1 + h]
        )
        cp.start()
        u_copies.append(cp)

    barrier = pltpu.get_barrier_semaphore()

    def greet(device):
        pl.semaphore_signal(barrier, inc=1, device_id=device, device_id_type=MESH)

    for k in range(1, NZ):
        greet(z_dev(k))
    for k in range(1, NX):
        greet(x_dev(k))
    for k in range(1, NY):
        greet(y_dev(k))
    greet(partner)

    had = hadamard_128()
    column_sign = (1 - 2 * sign_ref[...]).astype(F32)
    signed = (x_ref[...].astype(F32) * column_sign).astype(BF16)
    groups = butterfly(
        [
            jnp.dot(signed[:, g * 128 : (g + 1) * 128], had, preferred_element_type=F32)
            for g in range(4)
        ]
    )
    for a in range(4):
        for g in range(4):
            inner[a * 4 + g] = groups[g][a * 16 : (a + 1) * 16].astype(BF16)

    pl.semaphore_wait(barrier, NZ - 1 + NX - 1 + NY - 1 + 1)

    pending = []

    def send(src, dst, s_sem, r_sem, device):
        cp = pltpu.make_async_remote_copy(
            src_ref=src, dst_ref=dst, send_sem=s_sem, recv_sem=r_sem,
            device_id=device, device_id_type=MESH,
        )
        cp.start()
        pending.append(cp)

    def arrived(ref, sem):
        pltpu.make_async_remote_copy(
            src_ref=ref, dst_ref=ref, send_sem=sem, recv_sem=sem,
            device_id=partner, device_id_type=MESH,
        ).wait_recv()

    for k in range(1, NZ):
        j = lax.rem(me + k, NZ)
        send(inner.at[j], recv1.at[me], a1_send.at[k], a1_recv.at[k], z_dev(k))

    SIGN = (1, -1)
    HOPS = ((8, 7), (7, 8))

    def gather_step(s):
        for h in range(2):
            for way in range(2):
                sign = SIGN[way]
                if s > 0 and s - 1 < HOPS[way][h]:
                    rows = pl.ds(
                        pl.multiple_of(lax.rem(me - sign * s + NZ, NZ) * half, half), half
                    )
                    arrived(uall.at[h, rows], ag_recv.at[way, h, s - 1])
                if s < HOPS[way][h]:
                    rows = pl.ds(
                        pl.multiple_of(lax.rem(me - sign * s + NZ, NZ) * half, half), half
                    )
                    src = u_hbm.at[pl.ds(h * half, half)] if s == 0 else uall.at[h, rows]
                    send(
                        src, uall.at[h, rows],
                        ag_send.at[way, h, s], ag_recv.at[way, h, s], z_dev(sign),
                    )

    gather_step(0)

    recv1[me] = inner[me]
    for k in range(1, NZ):
        arrived(recv1.at[lax.rem(me - k + NZ, NZ)], a1_recv.at[k])
    factor = 1.0 / math.sqrt(8192.0)
    rotated = butterfly([recv1[t].astype(F32) for t in range(NZ)])
    for s in range(NZ):
        send2[s] = (rotated[s] * factor).astype(BF16)

    q_own = pl.ds(pl.multiple_of(chip * half, half), half)
    tile_rows = pl.ds(pl.multiple_of(chip * half + lax.div(me, 4) * 16, 16), 16)
    tile_cols = pl.ds(pl.multiple_of(lax.rem(me, 4) * 128, 128), 128)
    for k in range(1, NZ):
        j = lax.rem(me + k, NZ)
        send(
            send2.at[j], q.at[core, tile_rows, tile_cols],
            a2_send.at[k], a2_recv.at[k], z_dev(k),
        )
    own_tile = pltpu.make_async_copy(
        send2.at[me], q.at[core, tile_rows, tile_cols], loc_sem.at[3]
    )
    own_tile.start()

    gather_step(1)

    own_tile.wait()
    for k in range(1, NZ):
        arrived(send2.at[0], a2_recv.at[k])

    for k in range(1, NX):
        send(q.at[core, q_own], q.at[core, q_own], x_send.at[k], x_recv.at[k], x_dev(k))

    gather_step(2)

    def chip_rows(y, x):
        return pl.ds(pl.multiple_of((y * NX + x) * half, half), half)

    def line_rows(y):
        return pl.ds(pl.multiple_of(y * quarter, quarter), quarter)

    for k in range(1, NX):
        arrived(q.at[core, chip_rows(yy, lax.rem(xx - k + NX, NX))], x_recv.at[k])
    own_line = q.at[core, line_rows(yy)]
    for k in range(1, NY):
        send(own_line, own_line, y_send.at[k], y_recv.at[k], y_dev(k))
    send(own_line, own_line, c_send.at[0], c_recv.at[0], partner)

    gather_step(3)

    for k in range(1, NY):
        line = q.at[core, line_rows(lax.rem(yy - k + NY, NY))]
        arrived(line, y_recv.at[k])
        send(line, line, c_send.at[k], c_recv.at[k], partner)

    w_copy.wait()

    def products(c):
        @pl.loop(0, NY)
        def _(y):
            rows = line_rows(y)
            block = q[c, rows]
            part[c, rows] = jnp.dot(block, w[...], preferred_element_type=F32)
            columns = pl.ds(
                pl.multiple_of((c * NY + y) * quarter, quarter), quarter
            )
            qt[:, columns] = block.T

    products(core)
    gather_step(4)
    for k in range(NY):
        arrived(q.at[1 - core, line_rows(lax.rem(yy - k + NY, NY))], c_recv.at[k])
    products(1 - core)

    piece = half // SUB

    def reduce_step(s):
        for h in range(2):
            for r in range(SUB):
                for way in range(2):
                    sign = SIGN[way]
                    first = 8 - HOPS[way][h]
                    if s < first:
                        continue
                    e = lax.rem(me + sign * (8 - s) + NZ, NZ)
                    rows = pl.ds(pl.multiple_of(e * half + r * piece, piece), piece)
                    cut = pl.ds(r * piece, piece)
                    mine = part[h, rows]
                    if s == first:
                        src = sbuf.at[way, h, cut]
                        src[...] = mine.astype(BF16)
                    else:
                        src = rbuf.at[way, h, s - 1, cut]
                        arrived(src, rs_recv.at[way, h, r, s - 1])
                        src[...] = (src[...].astype(F32) + mine).astype(BF16)
                    send(
                        src, rbuf.at[way, h, s, cut],
                        rs_send.at[way, h, r, s], rs_recv.at[way, h, r, s], z_dev(sign),
                    )

    def grad_tile(i):
        rows = pl.ds(i * 128, 128)
        n = q.shape[1]
        grad_ref[rows, :] = jnp.dot(
            qt[rows, 0:n], uall[0], preferred_element_type=F32
        ) + jnp.dot(qt[rows, n : 2 * n], uall[1], preferred_element_type=F32)

    reduce_step(0)
    gather_step(5)
    reduce_step(1)
    gather_step(6)
    reduce_step(2)
    gather_step(7)
    reduce_step(3)
    gather_step(8)
    for cp in u_copies:
        cp.wait()
    for s in range(4, 8):
        reduce_step(s)
        grad_tile(s - 4)

    for h in range(2):
        for r in range(SUB):
            cut = pl.ds(r * piece, piece)
            total = part[h, pl.ds(pl.multiple_of(me * half + r * piece, piece), piece)]
            for way in range(2):
                src = rbuf.at[way, h, 7, cut]
                arrived(src, rs_recv.at[way, h, r, 7])
                total = total + src[...].astype(F32)
            proj_ref[pl.ds(h * half + r * piece, piece), :] = total.astype(BF16)

    for cp in pending:
        cp.wait_send()


def per_device(x_tokens, sign_bits, weight, upstream):
    tokens, width = x_tokens.shape
    hidden = weight.shape[1]
    half = tokens
    every = NZ * half
    dma = pltpu.SemaphoreType.DMA
    vmem = pl.BlockSpec(memory_space=pltpu.VMEM)
    anywhere = pl.BlockSpec(memory_space=pl.ANY)
    return pl.pallas_call(
        kernel,
        out_shape=(
            jax.ShapeDtypeStruct((2 * half, hidden), BF16),
            jax.ShapeDtypeStruct((width, hidden), F32),
        ),
        in_specs=[vmem, vmem, anywhere, anywhere],
        out_specs=(vmem, vmem),
        scratch_shapes=[
            pltpu.VMEM((16, 16, 128), BF16),
            pltpu.VMEM((16, 16, 128), BF16),
            pltpu.VMEM((16, 16, 128), BF16),
            pltpu.VMEM((2, every, width), BF16),
            pltpu.VMEM((width, 2 * every), BF16),
            pltpu.VMEM((width, hidden), BF16),
            pltpu.VMEM((2, every, hidden), BF16),
            pltpu.VMEM((2, every, hidden), F32),
            pltpu.VMEM((2, 2, 8, half, hidden), BF16),
            pltpu.VMEM((2, 2, half, hidden), BF16),
            dma((4,)),
            dma((NZ,)), dma((NZ,)), dma((NZ,)), dma((NZ,)),
            dma((NX,)), dma((NX,)), dma((NY,)), dma((NY,)), dma((NY,)), dma((NY,)),
            dma((2, 2, 8)), dma((2, 2, 8)),
            dma((2, 2, SUB, 8)), dma((2, 2, SUB, 8)),
        ],
        compiler_params=pltpu.CompilerParams(
            collective_id=0, has_side_effects=True, vmem_limit_bytes=48 << 20
        ),
    )(x_tokens, sign_bits.reshape(1, width), weight, upstream)


def solution(mesh):
    in_specs = (P("dp", "tensor"), P("tensor"), P("tensor", "dp"), P("tensor", "dp"))
    out_specs = (P("tensor", "dp"), P("tensor", "dp"))
    return jax.shard_map(
        per_device, mesh=mesh, in_specs=in_specs, out_specs=out_specs, check_vma=False
    )
```

```python
import math

import jax
import jax.numpy as jnp
from jax import lax
from jax.experimental import pallas as pl
from jax.experimental.pallas import tpu as pltpu
from jax.sharding import PartitionSpec as P

MESH = pl.DeviceIdType.MESH
F32 = jnp.float32
BF16 = jnp.bfloat16
NZ = 16
NX = 4
NY = 4
PARTS = 2


def hadamard_128():
    rows = lax.broadcasted_iota(jnp.int32, (128, 128), 0)
    cols = lax.broadcasted_iota(jnp.int32, (128, 128), 1)
    bits = rows & cols
    bits = bits ^ (bits >> 4)
    bits = bits ^ (bits >> 2)
    bits = bits ^ (bits >> 1)
    return (1 - 2 * (bits & 1)).astype(F32).astype(BF16)


def butterfly(values):
    values = list(values)
    stride = 1
    while stride < len(values):
        for low in range(len(values)):
            if not low & stride:
                a, b = values[low], values[low | stride]
                values[low], values[low | stride] = a + b, a - b
        stride *= 2
    return values


def kernel(
    x_hbm, sign_hbm, w_hbm, u_hbm, proj_ref, grad_ref,
    x_ref, sign_ref, inner, recv1, send2, q, qt, w, uall, part, rbuf, sbuf,
    loc_sem, a1_send, a1_recv, a2_send, a2_recv,
    x_send, x_recv, y_send, y_recv, c_send, c_recv,
    ag_send, ag_recv, rs_send, rs_recv,
):
    me = lax.axis_index("tensor")
    dp = lax.axis_index("dp")
    core = lax.rem(dp, 2)
    chip = lax.div(dp, 2)
    xx = lax.rem(chip, NX)
    yy = lax.div(chip, NX)
    part_rows = q.shape[4]

    def z_dev(shift):
        return {"tensor": lax.rem(me + shift + NZ, NZ)}

    def x_dev(shift):
        return {"dp": (yy * NX + lax.rem(xx + shift, NX)) * 2 + core}

    def y_dev(shift):
        return {"dp": (lax.rem(yy + shift, NY) * NX + xx) * 2 + core}

    partner = {"dp": chip * 2 + 1 - core}

    x_copy = pltpu.make_async_copy(x_hbm, x_ref, loc_sem.at[4])
    x_copy.start()
    sign_copy = pltpu.make_async_copy(sign_hbm, sign_ref, loc_sem.at[5])
    sign_copy.start()
    w_copy = pltpu.make_async_copy(w_hbm, w, loc_sem.at[0])
    w_copy.start()
    u_copies = []
    for h in range(2):
        cp = pltpu.make_async_copy(u_hbm.at[h], uall.at[h, :, me], loc_sem.at[1 + h])
        cp.start()
        u_copies.append(cp)

    barrier = pltpu.get_barrier_semaphore()

    def greet(device):
        pl.semaphore_signal(barrier, inc=1, device_id=device, device_id_type=MESH)

    for k in range(1, NZ):
        greet(z_dev(k))
    for k in range(1, NX):
        greet(x_dev(k))
    for k in range(1, NY):
        greet(y_dev(k))
    greet(partner)

    had = hadamard_128()
    x_copy.wait()
    sign_copy.wait()
    column_sign = (1 - 2 * sign_ref[...]).astype(F32)
    signed = (x_ref[...].astype(F32) * column_sign).astype(BF16)
    groups = butterfly(
        [
            jnp.dot(signed[:, g * 128 : (g + 1) * 128], had, preferred_element_type=F32)
            for g in range(4)
        ]
    )
    for a in range(4):
        for g in range(4):
            inner[a * 4 + g] = groups[g][a * 16 : (a + 1) * 16].astype(BF16)

    pl.semaphore_wait(barrier, NZ - 1 + NX - 1 + NY - 1 + 1)

    pending = []

    def send(src, dst, s_sem, r_sem, device):
        cp = pltpu.make_async_remote_copy(
            src_ref=src, dst_ref=dst, send_sem=s_sem, recv_sem=r_sem,
            device_id=device, device_id_type=MESH,
        )
        cp.start()
        pending.append(cp)

    def arrived(ref, sem):
        pltpu.make_async_remote_copy(
            src_ref=ref, dst_ref=ref, send_sem=sem, recv_sem=sem,
            device_id=partner, device_id_type=MESH,
        ).wait_recv()

    for k in range(1, NZ):
        j = lax.rem(me + k, NZ)
        send(inner.at[j], recv1.at[me], a1_send.at[k], a1_recv.at[k], z_dev(k))

    SIGN = (1, -1)
    HOPS = ((8, 7), (7, 8))

    def gather_step(s):
        for h in range(2):
            for way in range(2):
                sign = SIGN[way]
                chunk = uall.at[h, :, lax.rem(me - sign * s + NZ, NZ)]
                if s > 0 and s - 1 < HOPS[way][h]:
                    arrived(chunk, ag_recv.at[way, h, s - 1])
                if s < HOPS[way][h]:
                    send(
                        u_hbm.at[h] if s == 0 else chunk, chunk,
                        ag_send.at[way, h, s], ag_recv.at[way, h, s], z_dev(sign),
                    )

    gather_step(0)

    recv1[me] = inner[me]
    for k in range(1, NZ):
        arrived(recv1.at[lax.rem(me - k + NZ, NZ)], a1_recv.at[k])
    factor = 1.0 / math.sqrt(8192.0)
    rotated = butterfly([recv1[t].astype(F32) for t in range(NZ)])
    for s in range(NZ):
        send2[s] = (rotated[s] * factor).astype(BF16)

    block = lax.div(me, 4)
    tile = q.at[
        core, lax.div(block, 2), yy, xx,
        pl.ds(pl.multiple_of(lax.rem(block, 2) * 16, 16), 16),
        pl.ds(pl.multiple_of(lax.rem(me, 4) * 128, 128), 128),
    ]
    for k in range(1, NZ):
        j = lax.rem(me + k, NZ)
        send(send2.at[j], tile, a2_send.at[k], a2_recv.at[k], z_dev(k))
    own_tile = pltpu.make_async_copy(send2.at[me], tile, loc_sem.at[3])
    own_tile.start()

    gather_step(1)

    own_tile.wait()
    for k in range(1, NZ):
        arrived(send2.at[0], a2_recv.at[k])

    def x_from(k):
        return lax.rem(xx - k + NX, NX)

    def y_from(k):
        return lax.rem(yy - k + NY, NY)

    for k in range(1, NX):
        own = q.at[core, 0, yy, xx]
        send(own, own, x_send.at[0, k], x_recv.at[0, k], x_dev(k))
        own = q.at[core, 1, yy, xx]
        send(own, own, y_send.at[0, k], y_recv.at[0, k], y_dev(k))

    gather_step(2)

    for k in range(1, NX):
        arrived(q.at[core, 0, yy, x_from(k)], x_recv.at[0, k])
        arrived(q.at[core, 1, y_from(k), xx], y_recv.at[0, k])
    line = q.at[core, 0, yy]
    column = q.at[core, 1, :, xx]
    for k in range(1, NX):
        send(line, line, y_send.at[1, k], y_recv.at[1, k], y_dev(k))
        send(column, column, x_send.at[1, k], x_recv.at[1, k], x_dev(k))
    send(line, line, c_send.at[0, 0], c_recv.at[0, 0], partner)
    send(column, column, c_send.at[1, 0], c_recv.at[1, 0], partner)

    gather_step(3)
    gather_step(4)

    for k in range(1, NX):
        line = q.at[core, 0, y_from(k)]
        arrived(line, y_recv.at[1, k])
        send(line, line, c_send.at[0, k], c_recv.at[0, k], partner)
        column = q.at[core, 1, :, x_from(k)]
        arrived(column, x_recv.at[1, k])
        send(column, column, c_send.at[1, k], c_recv.at[1, k], partner)

    w_copy.wait()

    def products(c):
        @pl.loop(0, 2 * PARTS)
        def _(i):
            p, ys = lax.div(i, 2), pl.ds(lax.rem(i, 2) * 2, 2)
            rows = 2 * NX * part_rows
            tokens = q[c, p, ys].reshape(rows, q.shape[5])
            part[c, p, ys] = jnp.dot(
                tokens, w[...], preferred_element_type=F32
            ).reshape(2, NX, part_rows, w.shape[1])
            at = pl.multiple_of((c * 2 * PARTS + i) * rows, rows)
            qt[:, pl.ds(at, rows)] = tokens.T

    products(core)
    gather_step(5)
    for k in range(NX):
        arrived(q.at[1 - core, 0, y_from(k)], c_recv.at[0, k])
        arrived(q.at[1 - core, 1, :, x_from(k)], c_recv.at[1, k])
    products(1 - core)

    def reduce_step(s):
        for h in range(2):
            for p in range(PARTS):
                for way in range(2):
                    sign = SIGN[way]
                    first = 8 - HOPS[way][h]
                    if s < first:
                        continue
                    e = lax.rem(me + sign * (8 - s) + NZ, NZ)
                    mine = part[h, p, lax.div(e, NX), lax.rem(e, NX)]
                    if s == first:
                        src = sbuf.at[way, h, p]
                        src[...] = mine.astype(BF16)
                    else:
                        src = rbuf.at[way, h, p, s - 1]
                        arrived(src, rs_recv.at[way, h, p, s - 1])
                        src[...] = (src[...].astype(F32) + mine).astype(BF16)
                    send(
                        src, rbuf.at[way, h, p, s],
                        rs_send.at[way, h, p, s], rs_recv.at[way, h, p, s], z_dev(sign),
                    )

    def grad_tile(i):
        rows = pl.ds(i * 128, 128)
        n = qt.shape[1] // 2
        grad_ref[rows, :] = jnp.dot(
            qt[rows, 0:n], uall[0].reshape(n, w.shape[1]), preferred_element_type=F32
        ) + jnp.dot(
            qt[rows, n : 2 * n], uall[1].reshape(n, w.shape[1]), preferred_element_type=F32
        )

    reduce_step(0)
    gather_step(6)
    reduce_step(1)
    gather_step(7)
    reduce_step(2)
    gather_step(8)
    for cp in u_copies:
        cp.wait()
    for s in range(3, 8):
        reduce_step(s)
        if s < 7:
            grad_tile(s - 3)

    for h in range(2):
        for p in range(PARTS):
            total = part[h, p, lax.div(me, NX), lax.rem(me, NX)]
            for way in range(2):
                src = rbuf.at[way, h, p, 7]
                arrived(src, rs_recv.at[way, h, p, 7])
                total = total + src[...].astype(F32)
            proj_ref[pl.ds((h * PARTS + p) * part_rows, part_rows), :] = total.astype(BF16)

    for cp in pending:
        cp.wait_send()


def in_hbm(array):
    return pltpu.with_memory_space_constraint(array, pltpu.HBM)


def per_device(x_tokens, sign_bits, weight, upstream):
    tokens, width = x_tokens.shape
    hidden = weight.shape[1]
    rows = tokens // PARTS
    every = 2 * NZ * tokens
    dma = pltpu.SemaphoreType.DMA
    vmem = pl.BlockSpec(memory_space=pltpu.VMEM)
    anywhere = pl.BlockSpec(memory_space=pl.ANY)
    return pl.pallas_call(
        kernel,
        out_shape=(
            jax.ShapeDtypeStruct((2 * tokens, hidden), BF16),
            jax.ShapeDtypeStruct((width, hidden), F32),
        ),
        in_specs=[anywhere] * 4,
        out_specs=(vmem, vmem),
        scratch_shapes=[
            pltpu.VMEM((tokens, width), BF16),
            pltpu.VMEM((1, width), jnp.int32),
            pltpu.VMEM((16, 16, 128), BF16),
            pltpu.VMEM((16, 16, 128), BF16),
            pltpu.VMEM((16, 16, 128), BF16),
            pltpu.VMEM((2, PARTS, NY, NX, rows, width), BF16),
            pltpu.VMEM((width, every), BF16),
            pltpu.VMEM((width, hidden), BF16),
            pltpu.VMEM((2, PARTS, NZ, rows, hidden), BF16),
            pltpu.VMEM((2, PARTS, NY, NX, rows, hidden), F32),
            pltpu.VMEM((2, 2, PARTS, 8, rows, hidden), BF16),
            pltpu.VMEM((2, 2, PARTS, rows, hidden), BF16),
            dma((6,)),
            dma((NZ,)), dma((NZ,)), dma((NZ,)), dma((NZ,)),
            dma((2, NX)), dma((2, NX)), dma((2, NY)), dma((2, NY)), dma((2, NX)), dma((2, NX)),
            dma((2, 2, 8)), dma((2, 2, 8)),
            dma((2, 2, PARTS, 8)), dma((2, 2, PARTS, 8)),
        ],
        compiler_params=pltpu.CompilerParams(
            collective_id=0, has_side_effects=True, vmem_limit_bytes=48 << 20
        ),
    )(
        in_hbm(x_tokens),
        in_hbm(sign_bits.reshape(1, width)),
        in_hbm(weight),
        in_hbm(upstream.reshape(2, PARTS, rows, hidden)),
    )


def solution(mesh):
    in_specs = (P("dp", "tensor"), P("tensor"), P("tensor", "dp"), P("tensor", "dp"))
    out_specs = (P("tensor", "dp"), P("tensor", "dp"))
    return jax.shard_map(
        per_device, mesh=mesh, in_specs=in_specs, out_specs=out_specs, check_vma=False
    )
```

```python
import math

import jax
import jax.numpy as jnp
from jax import lax
from jax.experimental import pallas as pl
from jax.experimental.pallas import tpu as pltpu
from jax.sharding import PartitionSpec as P

MESH = pl.DeviceIdType.MESH
F32 = jnp.float32
BF16 = jnp.bfloat16
NZ = 16
NX = 4
NY = 4
FAR_FIRST = (8, 7, 9, 6, 10, 5, 11, 4, 12, 3, 13, 2, 14, 1, 15)
PARTS = 2


def hadamard_128():
    rows = lax.broadcasted_iota(jnp.int32, (128, 128), 0)
    cols = lax.broadcasted_iota(jnp.int32, (128, 128), 1)
    bits = rows & cols
    bits = bits ^ (bits >> 4)
    bits = bits ^ (bits >> 2)
    bits = bits ^ (bits >> 1)
    return (1 - 2 * (bits & 1)).astype(F32).astype(BF16)


def butterfly(values):
    values = list(values)
    stride = 1
    while stride < len(values):
        for low in range(len(values)):
            if not low & stride:
                a, b = values[low], values[low | stride]
                values[low], values[low | stride] = a + b, a - b
        stride *= 2
    return values


def kernel(
    x_hbm, sign_hbm, w_hbm, u_hbm, proj_ref, grad_ref,
    x_ref, sign_ref, inner, recv1, send2, recv2, q, qt, w, uall, part, rbuf, sbuf,
    loc_sem, a1_send, a1_recv, a2_send, a2_recv,
    x_send, x_recv, y_send, y_recv, c_send, c_recv,
    ag_send, ag_recv, rs_send, rs_recv,
):
    me = lax.axis_index("tensor")
    dp = lax.axis_index("dp")
    core = lax.rem(dp, 2)
    chip = lax.div(dp, 2)
    xx = lax.rem(chip, NX)
    yy = lax.div(chip, NX)
    part_rows = q.shape[4]

    def z_dev(shift):
        return {"tensor": lax.rem(me + shift + NZ, NZ)}

    def x_dev(shift):
        return {"dp": (yy * NX + lax.rem(xx + shift, NX)) * 2 + core}

    def y_dev(shift):
        return {"dp": (lax.rem(yy + shift, NY) * NX + xx) * 2 + core}

    partner = {"dp": chip * 2 + 1 - core}

    x_copy = pltpu.make_async_copy(x_hbm, x_ref, loc_sem.at[4])
    x_copy.start()
    sign_copy = pltpu.make_async_copy(sign_hbm, sign_ref, loc_sem.at[5])
    sign_copy.start()
    w_copy = pltpu.make_async_copy(w_hbm, w, loc_sem.at[0])
    w_copy.start()
    u_copies = []
    for h in range(2):
        cp = pltpu.make_async_copy(u_hbm.at[h], uall.at[h, :, me], loc_sem.at[1 + h])
        cp.start()
        u_copies.append(cp)

    barrier = pltpu.get_barrier_semaphore()

    def greet(device):
        pl.semaphore_signal(barrier, inc=1, device_id=device, device_id_type=MESH)

    for k in FAR_FIRST:
        greet(z_dev(k))
    for k in range(1, NX):
        greet(x_dev(k))
    for k in range(1, NY):
        greet(y_dev(k))
    greet(partner)

    had = hadamard_128()
    x_copy.wait()
    sign_copy.wait()
    column_sign = (1 - 2 * sign_ref[...]).astype(F32)
    signed = (x_ref[...].astype(F32) * column_sign).astype(BF16)
    groups = butterfly(
        [
            jnp.dot(signed[:, g * 128 : (g + 1) * 128], had, preferred_element_type=F32)
            for g in range(4)
        ]
    )
    for a in range(4):
        for g in range(4):
            inner[a * 4 + g] = groups[g][a * 16 : (a + 1) * 16].astype(BF16)

    pl.semaphore_wait(barrier, NZ - 1 + NX - 1 + NY - 1 + 1)

    pending = []

    def send(src, dst, s_sem, r_sem, device):
        cp = pltpu.make_async_remote_copy(
            src_ref=src, dst_ref=dst, send_sem=s_sem, recv_sem=r_sem,
            device_id=device, device_id_type=MESH,
        )
        cp.start()
        pending.append(cp)

    def arrived(ref, sem):
        pltpu.make_async_remote_copy(
            src_ref=ref, dst_ref=ref, send_sem=sem, recv_sem=sem,
            device_id=partner, device_id_type=MESH,
        ).wait_recv()

    for k in FAR_FIRST:
        j = lax.rem(me + k, NZ)
        send(inner.at[j], recv1.at[me], a1_send.at[k], a1_recv.at[k], z_dev(k))

    SIGN = (1, -1)
    HOPS = ((8, 7), (7, 8))

    def gather_step(s):
        for h in range(2):
            for way in range(2):
                sign = SIGN[way]
                chunk = uall.at[h, :, lax.rem(me - sign * s + NZ, NZ)]
                if s > 0 and s - 1 < HOPS[way][h]:
                    arrived(chunk, ag_recv.at[way, h, s - 1])
                if s < HOPS[way][h]:
                    send(
                        u_hbm.at[h] if s == 0 else chunk, chunk,
                        ag_send.at[way, h, s], ag_recv.at[way, h, s], z_dev(sign),
                    )

    gather_step(0)

    recv1[me] = inner[me]
    for k in range(1, NZ):
        arrived(recv1.at[lax.rem(me - k + NZ, NZ)], a1_recv.at[k])
    factor = 1.0 / math.sqrt(8192.0)
    rotated = butterfly([recv1[t].astype(F32) for t in range(NZ)])
    for s in range(NZ):
        send2[s] = (rotated[s] * factor).astype(BF16)

    for k in FAR_FIRST:
        j = lax.rem(me + k, NZ)
        send(send2.at[j], recv2.at[me], a2_send.at[k], a2_recv.at[k], z_dev(k))

    gather_step(1)

    recv2[me] = send2[me]
    for k in range(1, NZ):
        arrived(recv2.at[lax.rem(me - k + NZ, NZ)], a2_recv.at[k])
    for j in range(NZ):
        a, g = j // 4, j % 4
        row = a % 2 * 16
        q[core, a // 2, yy, xx, row : row + 16, g * 128 : (g + 1) * 128] = recv2[j]

    def x_from(k):
        return lax.rem(xx - k + NX, NX)

    def y_from(k):
        return lax.rem(yy - k + NY, NY)

    for k in range(1, NX):
        own = q.at[core, 0, yy, xx]
        send(own, own, x_send.at[0, k], x_recv.at[0, k], x_dev(k))
        own = q.at[core, 1, yy, xx]
        send(own, own, y_send.at[0, k], y_recv.at[0, k], y_dev(k))

    gather_step(2)

    for k in range(1, NX):
        arrived(q.at[core, 0, yy, x_from(k)], x_recv.at[0, k])
        arrived(q.at[core, 1, y_from(k), xx], y_recv.at[0, k])
    line = q.at[core, 0, yy]
    column = q.at[core, 1, :, xx]
    for k in range(1, NX):
        send(line, line, y_send.at[1, k], y_recv.at[1, k], y_dev(k))
        send(column, column, x_send.at[1, k], x_recv.at[1, k], x_dev(k))
    send(line, line, c_send.at[0, 0], c_recv.at[0, 0], partner)
    send(column, column, c_send.at[1, 0], c_recv.at[1, 0], partner)

    gather_step(3)
    gather_step(4)

    for k in range(1, NX):
        line = q.at[core, 0, y_from(k)]
        arrived(line, y_recv.at[1, k])
        send(line, line, c_send.at[0, k], c_recv.at[0, k], partner)
        column = q.at[core, 1, :, x_from(k)]
        arrived(column, x_recv.at[1, k])
        send(column, column, c_send.at[1, k], c_recv.at[1, k], partner)

    w_copy.wait()

    def products(c):
        @pl.loop(0, 2 * PARTS)
        def _(i):
            p, ys = lax.div(i, 2), pl.ds(lax.rem(i, 2) * 2, 2)
            rows = 2 * NX * part_rows
            tokens = q[c, p, ys].reshape(rows, q.shape[5])
            part[c, p, ys] = jnp.dot(
                tokens, w[...], preferred_element_type=F32
            ).reshape(2, NX, part_rows, w.shape[1])
            at = pl.multiple_of((c * 2 * PARTS + i) * rows, rows)
            qt[:, pl.ds(at, rows)] = tokens.T

    products(core)
    gather_step(5)
    for k in range(NX):
        arrived(q.at[1 - core, 0, y_from(k)], c_recv.at[0, k])
        arrived(q.at[1 - core, 1, :, x_from(k)], c_recv.at[1, k])
    products(1 - core)

    def reduce_step(s):
        for h in range(2):
            for p in range(PARTS):
                for way in range(2):
                    sign = SIGN[way]
                    first = 8 - HOPS[way][h]
                    if s < first:
                        continue
                    e = lax.rem(me + sign * (8 - s) + NZ, NZ)
                    mine = part[h, p, lax.div(e, NX), lax.rem(e, NX)]
                    if s == first:
                        src = sbuf.at[way, h, p]
                        src[...] = mine.astype(BF16)
                    else:
                        src = rbuf.at[way, h, p, s - 1]
                        arrived(src, rs_recv.at[way, h, p, s - 1])
                        src[...] = (src[...].astype(F32) + mine).astype(BF16)
                    send(
                        src, rbuf.at[way, h, p, s],
                        rs_send.at[way, h, p, s], rs_recv.at[way, h, p, s], z_dev(sign),
                    )

    def grad_tile(i):
        rows = pl.ds(i * 128, 128)
        n = qt.shape[1] // 2
        grad_ref[rows, :] = jnp.dot(
            qt[rows, 0:n], uall[0].reshape(n, w.shape[1]), preferred_element_type=F32
        ) + jnp.dot(
            qt[rows, n : 2 * n], uall[1].reshape(n, w.shape[1]), preferred_element_type=F32
        )

    reduce_step(0)
    gather_step(6)
    reduce_step(1)
    gather_step(7)
    reduce_step(2)
    gather_step(8)
    for cp in u_copies:
        cp.wait()
    for s in range(3, 8):
        reduce_step(s)
        if s < 7:
            grad_tile(s - 3)

    for h in range(2):
        for p in range(PARTS):
            total = part[h, p, lax.div(me, NX), lax.rem(me, NX)]
            for way in range(2):
                src = rbuf.at[way, h, p, 7]
                arrived(src, rs_recv.at[way, h, p, 7])
                total = total + src[...].astype(F32)
            proj_ref[pl.ds((h * PARTS + p) * part_rows, part_rows), :] = total.astype(BF16)

    for cp in pending:
        cp.wait_send()


def in_hbm(array):
    return pltpu.with_memory_space_constraint(array, pltpu.HBM)


def per_device(x_tokens, sign_bits, weight, upstream):
    tokens, width = x_tokens.shape
    hidden = weight.shape[1]
    rows = tokens // PARTS
    every = 2 * NZ * tokens
    dma = pltpu.SemaphoreType.DMA
    vmem = pl.BlockSpec(memory_space=pltpu.VMEM)
    anywhere = pl.BlockSpec(memory_space=pl.ANY)
    return pl.pallas_call(
        kernel,
        out_shape=(
            jax.ShapeDtypeStruct((2 * tokens, hidden), BF16),
            jax.ShapeDtypeStruct((width, hidden), F32),
        ),
        in_specs=[anywhere] * 4,
        out_specs=(vmem, vmem),
        scratch_shapes=[
            pltpu.VMEM((tokens, width), BF16),
            pltpu.VMEM((1, width), jnp.int32),
            pltpu.VMEM((16, 16, 128), BF16),
            pltpu.VMEM((16, 16, 128), BF16),
            pltpu.VMEM((16, 16, 128), BF16),
            pltpu.VMEM((16, 16, 128), BF16),
            pltpu.VMEM((2, PARTS, NY, NX, rows, width), BF16),
            pltpu.VMEM((width, every), BF16),
            pltpu.VMEM((width, hidden), BF16),
            pltpu.VMEM((2, PARTS, NZ, rows, hidden), BF16),
            pltpu.VMEM((2, PARTS, NY, NX, rows, hidden), F32),
            pltpu.VMEM((2, 2, PARTS, 8, rows, hidden), BF16),
            pltpu.VMEM((2, 2, PARTS, rows, hidden), BF16),
            dma((6,)),
            dma((NZ,)), dma((NZ,)), dma((NZ,)), dma((NZ,)),
            dma((2, NX)), dma((2, NX)), dma((2, NY)), dma((2, NY)), dma((2, NX)), dma((2, NX)),
            dma((2, 2, 8)), dma((2, 2, 8)),
            dma((2, 2, PARTS, 8)), dma((2, 2, PARTS, 8)),
        ],
        compiler_params=pltpu.CompilerParams(
            collective_id=0, has_side_effects=True, vmem_limit_bytes=48 << 20
        ),
    )(
        in_hbm(x_tokens),
        in_hbm(sign_bits.reshape(1, width)),
        in_hbm(weight),
        in_hbm(upstream.reshape(2, PARTS, rows, hidden)),
    )


def solution(mesh):
    in_specs = (P("dp", "tensor"), P("tensor"), P("tensor", "dp"), P("tensor", "dp"))
    out_specs = (P("tensor", "dp"), P("tensor", "dp"))
    return jax.shard_map(
        per_device, mesh=mesh, in_specs=in_specs, out_specs=out_specs, check_vma=False
    )
```

```python
import math

import jax
import jax.numpy as jnp
from jax import lax
from jax.experimental import pallas as pl
from jax.experimental.pallas import tpu as pltpu
from jax.sharding import PartitionSpec as P

MESH = pl.DeviceIdType.MESH
F32 = jnp.float32
BF16 = jnp.bfloat16
NZ = 16
NX = 4
NY = 4
FAR_FIRST = (8, 7, 9, 6, 10, 5, 11, 4, 12, 3, 13, 2, 14, 1, 15)
PARTS = 2


def hadamard_128():
    rows = lax.broadcasted_iota(jnp.int32, (128, 128), 0)
    cols = lax.broadcasted_iota(jnp.int32, (128, 128), 1)
    bits = rows & cols
    bits = bits ^ (bits >> 4)
    bits = bits ^ (bits >> 2)
    bits = bits ^ (bits >> 1)
    return (1 - 2 * (bits & 1)).astype(F32).astype(BF16)


def butterfly(values):
    values = list(values)
    stride = 1
    while stride < len(values):
        for low in range(len(values)):
            if not low & stride:
                a, b = values[low], values[low | stride]
                values[low], values[low | stride] = a + b, a - b
        stride *= 2
    return values


def kernel(
    x_hbm, sign_hbm, w_hbm, u_hbm, proj_ref, grad_ref,
    x_ref, sign_ref, inner, recv1, send2, recv2, q, qt, w, uall, part, rbuf, sbuf,
    loc_sem, a1_send, a1_recv, a2_send, a2_recv,
    x_send, x_recv, y_send, y_recv, c_send, c_recv,
    ag_send, ag_recv, rs_send, rs_recv,
):
    me = lax.axis_index("tensor")
    dp = lax.axis_index("dp")
    core = lax.rem(dp, 2)
    chip = lax.div(dp, 2)
    xx = lax.rem(chip, NX)
    yy = lax.div(chip, NX)
    part_rows = q.shape[4]

    def z_dev(shift):
        return {"tensor": lax.rem(me + shift + NZ, NZ)}

    def x_dev(shift):
        return {"dp": (yy * NX + lax.rem(xx + shift, NX)) * 2 + core}

    def y_dev(shift):
        return {"dp": (lax.rem(yy + shift, NY) * NX + xx) * 2 + core}

    partner = {"dp": chip * 2 + 1 - core}

    x_copy = pltpu.make_async_copy(x_hbm, x_ref, loc_sem.at[4])
    x_copy.start()
    sign_copy = pltpu.make_async_copy(sign_hbm, sign_ref, loc_sem.at[5])
    sign_copy.start()
    barrier = pltpu.get_barrier_semaphore()

    def greet(device):
        pl.semaphore_signal(barrier, inc=1, device_id=device, device_id_type=MESH)

    for k in FAR_FIRST:
        greet(z_dev(k))
    for k in range(1, NX):
        greet(x_dev(k))
    for k in range(1, NY):
        greet(y_dev(k))
    greet(partner)

    had = hadamard_128()
    x_copy.wait()
    sign_copy.wait()
    column_sign = (1 - 2 * sign_ref[...]).astype(F32)
    signed = (x_ref[...].astype(F32) * column_sign).astype(BF16)
    groups = butterfly(
        [
            jnp.dot(signed[:, g * 128 : (g + 1) * 128], had, preferred_element_type=F32)
            for g in range(4)
        ]
    )
    for a in range(4):
        for g in range(4):
            inner[a * 4 + g] = groups[g][a * 16 : (a + 1) * 16].astype(BF16)

    pl.semaphore_wait(barrier, NZ - 1 + NX - 1 + NY - 1 + 1)

    pending = []

    def send(src, dst, s_sem, r_sem, device):
        cp = pltpu.make_async_remote_copy(
            src_ref=src, dst_ref=dst, send_sem=s_sem, recv_sem=r_sem,
            device_id=device, device_id_type=MESH,
        )
        cp.start()
        pending.append(cp)

    def arrived(ref, sem):
        pltpu.make_async_remote_copy(
            src_ref=ref, dst_ref=ref, send_sem=sem, recv_sem=sem,
            device_id=partner, device_id_type=MESH,
        ).wait_recv()

    for k in FAR_FIRST:
        j = lax.rem(me + k, NZ)
        send(inner.at[j], recv1.at[me], a1_send.at[k], a1_recv.at[k], z_dev(k))

    SIGN = (1, -1)
    HOPS = ((8, 7), (7, 8))

    def gather_step(s):
        for h in range(2):
            for way in range(2):
                sign = SIGN[way]
                chunk = uall.at[h, :, lax.rem(me - sign * s + NZ, NZ)]
                if s > 0 and s - 1 < HOPS[way][h]:
                    arrived(chunk, ag_recv.at[way, h, s - 1])
                if s < HOPS[way][h]:
                    send(
                        u_hbm.at[h] if s == 0 else chunk, chunk,
                        ag_send.at[way, h, s], ag_recv.at[way, h, s], z_dev(sign),
                    )

    gather_step(0)
    w_copy = pltpu.make_async_copy(w_hbm, w, loc_sem.at[0])
    w_copy.start()
    u_copies = []
    for h in range(2):
        cp = pltpu.make_async_copy(u_hbm.at[h], uall.at[h, :, me], loc_sem.at[1 + h])
        cp.start()
        u_copies.append(cp)


    recv1[me] = inner[me]
    for k in range(1, NZ):
        arrived(recv1.at[lax.rem(me - k + NZ, NZ)], a1_recv.at[k])
    factor = 1.0 / math.sqrt(8192.0)
    rotated = butterfly([recv1[t].astype(F32) for t in range(NZ)])
    for s in range(NZ):
        send2[s] = (rotated[s] * factor).astype(BF16)

    for k in FAR_FIRST:
        j = lax.rem(me + k, NZ)
        send(send2.at[j], recv2.at[me], a2_send.at[k], a2_recv.at[k], z_dev(k))

    gather_step(1)

    recv2[me] = send2[me]
    for k in range(1, NZ):
        arrived(recv2.at[lax.rem(me - k + NZ, NZ)], a2_recv.at[k])
    for j in range(NZ):
        a, g = j // 4, j % 4
        row = a % 2 * 16
        q[core, a // 2, yy, xx, row : row + 16, g * 128 : (g + 1) * 128] = recv2[j]

    def x_from(k):
        return lax.rem(xx - k + NX, NX)

    def y_from(k):
        return lax.rem(yy - k + NY, NY)

    for k in range(1, NX):
        own = q.at[core, 0, yy, xx]
        send(own, own, x_send.at[0, k], x_recv.at[0, k], x_dev(k))
        own = q.at[core, 1, yy, xx]
        send(own, own, y_send.at[0, k], y_recv.at[0, k], y_dev(k))

    gather_step(2)

    for k in range(1, NX):
        arrived(q.at[core, 0, yy, x_from(k)], x_recv.at[0, k])
        arrived(q.at[core, 1, y_from(k), xx], y_recv.at[0, k])
    line = q.at[core, 0, yy]
    column = q.at[core, 1, :, xx]
    for k in range(1, NX):
        send(line, line, y_send.at[1, k], y_recv.at[1, k], y_dev(k))
        send(column, column, x_send.at[1, k], x_recv.at[1, k], x_dev(k))
    send(line, line, c_send.at[0, 0], c_recv.at[0, 0], partner)
    send(column, column, c_send.at[1, 0], c_recv.at[1, 0], partner)

    gather_step(3)
    gather_step(4)

    for k in range(1, NX):
        line = q.at[core, 0, y_from(k)]
        arrived(line, y_recv.at[1, k])
        send(line, line, c_send.at[0, k], c_recv.at[0, k], partner)
        column = q.at[core, 1, :, x_from(k)]
        arrived(column, x_recv.at[1, k])
        send(column, column, c_send.at[1, k], c_recv.at[1, k], partner)

    w_copy.wait()

    def products(c):
        @pl.loop(0, 2 * PARTS)
        def _(i):
            p, ys = lax.div(i, 2), pl.ds(lax.rem(i, 2) * 2, 2)
            rows = 2 * NX * part_rows
            tokens = q[c, p, ys].reshape(rows, q.shape[5])
            part[c, p, ys] = jnp.dot(
                tokens, w[...], preferred_element_type=F32
            ).reshape(2, NX, part_rows, w.shape[1])
            at = pl.multiple_of((c * 2 * PARTS + i) * rows, rows)
            qt[:, pl.ds(at, rows)] = tokens.T

    products(core)
    gather_step(5)
    for k in range(NX):
        arrived(q.at[1 - core, 0, y_from(k)], c_recv.at[0, k])
        arrived(q.at[1 - core, 1, :, x_from(k)], c_recv.at[1, k])
    products(1 - core)

    def reduce_step(s):
        for h in range(2):
            for p in range(PARTS):
                for way in range(2):
                    sign = SIGN[way]
                    first = 8 - HOPS[way][h]
                    if s < first:
                        continue
                    e = lax.rem(me + sign * (8 - s) + NZ, NZ)
                    mine = part[h, p, lax.div(e, NX), lax.rem(e, NX)]
                    if s == first:
                        src = sbuf.at[way, h, p]
                        src[...] = mine.astype(BF16)
                    else:
                        src = rbuf.at[way, h, p, s - 1]
                        arrived(src, rs_recv.at[way, h, p, s - 1])
                        src[...] = (src[...].astype(F32) + mine).astype(BF16)
                    send(
                        src, rbuf.at[way, h, p, s],
                        rs_send.at[way, h, p, s], rs_recv.at[way, h, p, s], z_dev(sign),
                    )

    def grad_tile(i):
        rows = pl.ds(i * 128, 128)
        n = qt.shape[1] // 2
        grad_ref[rows, :] = jnp.dot(
            qt[rows, 0:n], uall[0].reshape(n, w.shape[1]), preferred_element_type=F32
        ) + jnp.dot(
            qt[rows, n : 2 * n], uall[1].reshape(n, w.shape[1]), preferred_element_type=F32
        )

    reduce_step(0)
    gather_step(6)
    reduce_step(1)
    reduce_step(2)
    gather_step(7)
    reduce_step(3)
    reduce_step(4)
    gather_step(8)
    for cp in u_copies:
        cp.wait()
    reduce_step(5)
    grad_tile(0)
    reduce_step(6)
    grad_tile(1)
    grad_tile(2)
    reduce_step(7)
    grad_tile(3)

    for h in range(2):
        for p in range(PARTS):
            total = part[h, p, lax.div(me, NX), lax.rem(me, NX)]
            for way in range(2):
                src = rbuf.at[way, h, p, 7]
                arrived(src, rs_recv.at[way, h, p, 7])
                total = total + src[...].astype(F32)
            proj_ref[pl.ds((h * PARTS + p) * part_rows, part_rows), :] = total.astype(BF16)

    for cp in pending:
        cp.wait_send()


def in_hbm(array):
    return pltpu.with_memory_space_constraint(array, pltpu.HBM)


def per_device(x_tokens, sign_bits, weight, upstream):
    tokens, width = x_tokens.shape
    hidden = weight.shape[1]
    rows = tokens // PARTS
    every = 2 * NZ * tokens
    dma = pltpu.SemaphoreType.DMA
    vmem = pl.BlockSpec(memory_space=pltpu.VMEM)
    anywhere = pl.BlockSpec(memory_space=pl.ANY)
    return pl.pallas_call(
        kernel,
        out_shape=(
            jax.ShapeDtypeStruct((2 * tokens, hidden), BF16),
            jax.ShapeDtypeStruct((width, hidden), F32),
        ),
        in_specs=[anywhere] * 4,
        out_specs=(vmem, vmem),
        scratch_shapes=[
            pltpu.VMEM((tokens, width), BF16),
            pltpu.VMEM((1, width), jnp.int32),
            pltpu.VMEM((16, 16, 128), BF16),
            pltpu.VMEM((16, 16, 128), BF16),
            pltpu.VMEM((16, 16, 128), BF16),
            pltpu.VMEM((16, 16, 128), BF16),
            pltpu.VMEM((2, PARTS, NY, NX, rows, width), BF16),
            pltpu.VMEM((width, every), BF16),
            pltpu.VMEM((width, hidden), BF16),
            pltpu.VMEM((2, PARTS, NZ, rows, hidden), BF16),
            pltpu.VMEM((2, PARTS, NY, NX, rows, hidden), F32),
            pltpu.VMEM((2, 2, PARTS, 8, rows, hidden), BF16),
            pltpu.VMEM((2, 2, PARTS, rows, hidden), BF16),
            dma((6,)),
            dma((NZ,)), dma((NZ,)), dma((NZ,)), dma((NZ,)),
            dma((2, NX)), dma((2, NX)), dma((2, NY)), dma((2, NY)), dma((2, NX)), dma((2, NX)),
            dma((2, 2, 8)), dma((2, 2, 8)),
            dma((2, 2, PARTS, 8)), dma((2, 2, PARTS, 8)),
        ],
        compiler_params=pltpu.CompilerParams(
            collective_id=0, has_side_effects=True, vmem_limit_bytes=48 << 20
        ),
    )(
        in_hbm(x_tokens),
        in_hbm(sign_bits.reshape(1, width)),
        in_hbm(weight),
        in_hbm(upstream.reshape(2, PARTS, rows, hidden)),
    )


def solution(mesh):
    in_specs = (P("dp", "tensor"), P("tensor"), P("tensor", "dp"), P("tensor", "dp"))
    out_specs = (P("tensor", "dp"), P("tensor", "dp"))
    return jax.shard_map(
        per_device, mesh=mesh, in_specs=in_specs, out_specs=out_specs, check_vma=False
    )
```
